32 devices in a mesh: band: 4 (over y, core), pgroup: 8 (over z, x).
Axes of the slice: x: 2, y: 2, z: 4, core: 2. Of those that a mesh axis runs over, the one named last changes fastest.
Arguments:
- state: float32 [128, 256, 512], P('pgroup', 'band'), may hold values from -6 to 6
- forcing: float32 [256, 512], P('band'), may hold values from -3 to 3
- parents: int32 [64, 128], P('band'), may hold values from 0 to 127, as said below
- taper_index: int32 [256], P('band'), may hold values from 0 to 7
Outputs:
- analysis: float32 [128, 256, 512], P('pgroup', 'band')
The draws below stay inside these ranges and needn't reach their ends.
Inputs may be any that keep to these rules, and one draw needn't show every extreme that they name: In every patch, the parents of the 16 particles k with k // 16 = g are distinct and come from exactly 8 groups (a group holds the particles j with the same j // 16), exactly 2 from each of them, for every patch and every g.
All inputs are finite; a program needn't handle non-finite values.
Results may differ from the reference program's by a relative error of at most 0.000071.
Values sent between devices are 32-bit elements; how exact they have to be, the bound alone decides.
A program may use at most 64 MiB of HBM per device.

```python
import jax
import jax.numpy as jnp
from jax import lax

NX = 512
PART_DEV = 16
PATCH_ROWS = 4
STEPS = 6
CAP = 2
NY = 256
PARTICLES = 128
PATCHES = 64


def draw_parents(key, part):
    groups = PARTICLES // PART_DEV
    sources = PART_DEV // CAP
    pairs = PATCHES * groups
    key_src, key_loc, key_mix = jax.random.split(key, 3)
    chosen_src = jax.vmap(lambda k: jax.random.permutation(k, groups))(jax.random.split(key_src, pairs))[:, :sources]
    chosen_loc = jax.vmap(lambda k: jax.random.permutation(k, PART_DEV))(jax.random.split(key_loc, pairs * sources)).reshape(pairs, sources, PART_DEV)
    slot = jnp.arange(PART_DEV, dtype=jnp.int32)
    position = slot // CAP
    order = slot % CAP
    owner = chosen_src[:, position]
    within = chosen_loc[:, position, order]
    parent = owner * PART_DEV + within
    shuffle = jax.vmap(lambda k: jax.random.permutation(k, PART_DEV))(jax.random.split(key_mix, pairs))
    parent = jnp.take_along_axis(parent, shuffle, axis=1)
    return parent.reshape(PATCHES, groups * PART_DEV).astype(jnp.int32)


def touch_ends(entries, rng, least, top_value):
    longest = entries.shape.index(max(entries.shape))
    spots = []
    for shift in (0, 1):
        where = [jax.random.randint(jax.random.fold_in(rng, axis), (), 0, length) for axis, length in enumerate(entries.shape)]
        where[longest] = (where[longest] + shift) % entries.shape[longest]
        spots.append(tuple(where))
    return entries.at[spots[0]].set(least).at[spots[1]].set(top_value)


def block_scale(rng, extent, pieces, least, high):
    level, own = 1.0, jax.random.fold_in(rng, 6)
    for dim, blocks in pieces:
        heights = jnp.exp(jax.random.uniform(jax.random.fold_in(own, dim), (blocks,), jnp.float32, least / len(pieces), high / len(pieces)))
        level = level * jnp.repeat(heights, extent[dim] // blocks).reshape([-1 if axis == dim else 1 for axis in range(len(extent))])
    return level


def normal_values(own_key, shape, deviation, reach, cuts=(), kind=jnp.bfloat16):
    drawn = deviation * jax.random.normal(own_key, shape, jnp.float32)
    if cuts:
        drawn = drawn * block_scale(own_key, shape, cuts, -0.22, 0.18)
    return jnp.clip(drawn, -reach, reach).astype(kind)


def setup_inputs(seed: int = 0) -> dict:
    arg_keys = jax.random.split(jax.random.key(seed), 5)
    state = normal_values(arg_keys[0], (PARTICLES, NY, NX), 1.0, 6.0, ((0, 8), (1, 4)), jnp.float32)
    forcing = normal_values(arg_keys[1], (NY, NX), 0.3, 3.0, ((0, 4),), jnp.float32)
    parents = draw_parents(jax.random.fold_in(arg_keys[4], 71), 0)
    taper_index = touch_ends(jax.random.randint(arg_keys[3], (NY,), 0, 8), jax.random.fold_in(arg_keys[3], 1), 0, 7).astype(jnp.int32)
    return {"state": state, "forcing": forcing, "parents": parents, "taper_index": taper_index}


advect_x = 0.05
advect_y = 0.1
diffuse = 0.15
taper_kinds = 8


def advect(padded, drive):
    center = padded[:, 1:-1]
    north = padded[:, 2:]
    south = padded[:, :-2]
    east = jnp.roll(center, -1, axis=2)
    west = jnp.roll(center, 1, axis=2)
    return center - advect_x * center * (east - west) - advect_y * (north - south) + diffuse * (east + west + north + south - 4.0 * center) + drive[None]


def taper_weights(taper_rows):
    offsets = jnp.arange(5, dtype=jnp.float32) - 2.0
    rates = 0.2 * (jnp.arange(taper_kinds, dtype=jnp.float32) + 1.0)
    raw_table = jnp.exp(-rates[:, None] * offsets[None, :] * offsets[None, :])
    table = raw_table / jnp.sum(raw_table, axis=1, keepdims=True)
    onehot = (taper_rows[:, None] == jnp.arange(taper_kinds, dtype=jnp.int32)[None, :]).astype(jnp.float32)
    return jnp.dot(onehot, table, precision=lax.Precision.HIGHEST)


def blend(padded, weights):
    rows = weights.shape[0]
    total = weights[:, 0][None, :, None] * padded[:, 0:rows]
    for offset in range(1, 5):
        total = total + weights[:, offset][None, :, None] * padded[:, offset:offset + rows]
    return total


def reference(state, forcing, parents, taper_index):
    field = state
    for repeat in range(STEPS):
        field = advect(jnp.pad(field, ((0, 0), (1, 1), (0, 0))), forcing)
    blocks = field.reshape(PARTICLES, PATCHES, PATCH_ROWS * NX)
    picked = blocks[parents.T, jnp.arange(PATCHES, dtype=jnp.int32)[None, :]]
    field = picked.reshape(PARTICLES, NY, NX)
    field = blend(jnp.pad(field, ((0, 0), (2, 2), (0, 0))), taper_weights(taper_index))
    for repeat in range(STEPS):
        field = advect(jnp.pad(field, ((0, 0), (1, 1), (0, 0))), forcing)
    return field
```

```python
import functools

import jax
import jax.numpy as jnp
from jax import lax
from jax.experimental import pallas as pl
from jax.experimental.pallas import tpu as pltpu
from jax.sharding import PartitionSpec as P

PATCH_ROWS = 4
STEPS = 6
CAP = 2
TILE = 8
MESH = pl.DeviceIdType.MESH


def advance(v, drive, above_ok, below_ok):
    rows, width = v.shape
    v = zero_outside(v, above_ok, below_ok)
    for _ in range(STEPS):
        east = pltpu.roll(v, width - 1, 1)
        west = pltpu.roll(v, 1, 1)
        north = pltpu.roll(v, rows - 1, 0)
        south = pltpu.roll(v, 1, 0)
        v = (
            v * (0.4 - 0.05 * (east - west))
            + (0.15 * (east + west) + drive)
            + (0.05 * north + 0.25 * south)
        )
        v = zero_outside(v, above_ok, below_ok)
    return v


def zero_outside(v, above_ok, below_ok):
    if above_ok is not None:
        v = jnp.concatenate([jnp.where(above_ok, v[:TILE], 0.0), v[TILE:]], axis=0)
    if below_ok is not None:
        v = jnp.concatenate([v[:-TILE], jnp.where(below_ok, v[-TILE:], 0.0)], axis=0)
    return v


def window(low, mid, high, pick, start, rows):
    extent = mid.shape[-2]
    begin, end = start - TILE, start + rows + TILE
    parts = []
    if begin < 0:
        parts.append(low[pick + (slice(None), slice(None))])
    parts.append(mid[pick + (slice(max(begin, 0), min(end, extent)), slice(None))])
    if end > extent:
        parts.append(high[pick + (slice(None), slice(None))])
    return jnp.concatenate(parts, axis=0) if len(parts) > 1 else parts[0]


def kernel(
    bands, groups, chunks, jobs1, jobs2,
    state, forcing, taper, chosen, picks, out,
    first, resampled,
    s_lo, s_hi, f_lo, f_hi, t_lo, t_hi, r_lo, r_hi,
    halo_send, halo_recv, send_sem, recv_sem, own_sem,
    *buffers,
):
    count = len(chunks)
    sends, recvs = buffers[:count], buffers[count:]
    band = lax.axis_index("band")
    me = lax.axis_index("pgroup")
    per_dev, extent, width = state.shape
    has_low, has_high = band > 0, band < bands - 1
    up, down = lax.rem(band + 1, bands), lax.rem(band + bands - 1, bands)

    barrier = pltpu.get_barrier_semaphore()
    for step in range(1, groups):
        pl.semaphore_signal(
            barrier, inc=1, device_id={"pgroup": lax.rem(me + step, groups)}, device_id_type=MESH
        )

    @pl.when(has_low)
    def _():
        pl.semaphore_signal(barrier, inc=1, device_id={"band": down}, device_id_type=MESH)

    @pl.when(has_high)
    def _():
        pl.semaphore_signal(barrier, inc=1, device_id={"band": up}, device_id_type=MESH)

    def halo(index, src, low, high):
        lead = (slice(None),) * (len(src.shape) - 2)
        upward = pltpu.make_async_remote_copy(
            src_ref=src.at[lead + (slice(extent - TILE, extent),)], dst_ref=low,
            send_sem=halo_send.at[2 * index], recv_sem=halo_recv.at[2 * index],
            device_id={"band": up}, device_id_type=MESH,
        )
        downward = pltpu.make_async_remote_copy(
            src_ref=src.at[lead + (slice(0, TILE),)], dst_ref=high,
            send_sem=halo_send.at[2 * index + 1], recv_sem=halo_recv.at[2 * index + 1],
            device_id={"band": down}, device_id_type=MESH,
        )
        return upward, downward

    edges = [
        halo(0, state, s_lo, s_hi),
        halo(1, forcing, f_lo, f_hi),
        halo(2, taper, t_lo, t_hi),
    ]
    middle = halo(3, resampled, r_lo, r_hi)

    @pl.when(jnp.logical_not(has_low))
    def _():
        for ref in (s_lo, f_lo, t_lo, r_lo):
            ref[...] = jnp.zeros_like(ref)

    @pl.when(jnp.logical_not(has_high))
    def _():
        for ref in (s_hi, f_hi, t_hi, r_hi):
            ref[...] = jnp.zeros_like(ref)

    def bounds(start, rows):
        return (
            has_low if start < TILE else None,
            has_high if start + rows + TILE > extent else None,
        )

    def before(start, rows):
        above_ok, below_ok = bounds(start, rows)

        def body(k, carry):
            v = window(s_lo, state, s_hi, (k,), start, rows)
            drive = window(f_lo, forcing, f_hi, (), start, rows)
            v = advance(v, drive, above_ok, below_ok)
            first[k, pl.ds(start, rows), :] = v[TILE : TILE + rows]
            return carry

        lax.fori_loop(0, per_dev, body, 0)

    def after(start, rows):
        above_ok, below_ok = bounds(start, rows)
        kind = window(t_lo, taper, t_hi, (), start, rows) + 1.0
        near, far = jnp.exp(-0.2 * kind), jnp.exp(-0.8 * kind)
        scale = 1.0 / (1.0 + 2.0 * near + 2.0 * far)
        repeat = width // taper.shape[1]
        w0, w1, w2 = (
            jnp.concatenate([w] * repeat, axis=1) for w in (scale, near * scale, far * scale)
        )

        def body(k, carry):
            v = window(r_lo, resampled, r_hi, (k,), start, rows)
            full = v.shape[0]
            drive = window(f_lo, forcing, f_hi, (), start, rows)
            v = (
                w0 * v
                + w1 * (pltpu.roll(v, 1, 0) + pltpu.roll(v, full - 1, 0))
                + w2 * (pltpu.roll(v, 2, 0) + pltpu.roll(v, full - 2, 0))
            )
            v = advance(v, drive, above_ok, below_ok)
            out[k, pl.ds(start, rows), :] = v[TILE : TILE + rows]
            return carry

        lax.fori_loop(0, per_dev, body, 0)

    shifts = sorted(range(1, groups), key=lambda i: -min(i, groups - i))

    def exchange(index):
        copies = []
        for shift in shifts:
            copies.append(
                pltpu.make_async_remote_copy(
                    src_ref=sends[index].at[lax.rem(me + shift, groups)],
                    dst_ref=recvs[index].at[me],
                    send_sem=send_sem.at[index, shift - 1],
                    recv_sem=recv_sem.at[index, shift - 1],
                    device_id={"pgroup": lax.rem(me + shift, groups)},
                    device_id_type=MESH,
                )
            )
        own = pltpu.make_async_copy(sends[index].at[me], recvs[index].at[me], own_sem.at[index])
        return copies, own

    upper = lax.broadcasted_iota(jnp.int32, (TILE, width), 0) < PATCH_ROWS

    def gather(index):
        base, tiles = chunks[index]
        send = sends[index]

        def body(g, carry):
            for j in range(tiles):
                rows = pl.ds((base + j) * TILE, TILE)
                for slot in range(CAP):
                    at = ((2 * (base + j)) * groups + g) * CAP + slot
                    even, odd = chosen[at], chosen[at + groups * CAP]
                    send[g, j, slot] = jnp.where(upper, first[even, rows, :], first[odd, rows, :])
            return carry

        lax.fori_loop(0, groups, body, 0)

    def scatter(index):
        base, tiles = chunks[index]
        recv = recvs[index]

        def body(k, carry):
            for j in range(tiles):
                at = ((2 * (base + j)) * per_dev + k) * 2
                even = recv[picks[at], j, picks[at + 1]]
                odd = recv[picks[at + 2 * per_dev], j, picks[at + 2 * per_dev + 1]]
                resampled[k, pl.ds((base + j) * TILE, TILE), :] = jnp.where(upper, even, odd)
            return carry

        lax.fori_loop(0, per_dev, body, 0)

    plans = [exchange(index) for index in range(count)]
    for index in range(count):
        for start, rows in jobs1[index]:
            before(start, rows)
        gather(index)
        if index == 0:
            pl.semaphore_wait(
                barrier, groups - 1 + has_low.astype(jnp.int32) + has_high.astype(jnp.int32)
            )

            @pl.when(has_high)
            def _():
                for upward, _ in edges:
                    upward.start()

            @pl.when(has_low)
            def _():
                for _, downward in edges:
                    downward.start()

        copies, own = plans[index]
        for copy in copies:
            copy.start()
        own.start()
        if index == 0:

            @pl.when(has_low)
            def _():
                for upward, _ in edges:
                    upward.wait_recv()

            @pl.when(has_high)
            def _():
                for _, downward in edges:
                    downward.wait_recv()

    for index in range(count):
        copies, own = plans[index]
        for copy in copies:
            copy.wait_recv()
        own.wait()
        scatter(index)
        base, tiles = chunks[index]
        if base == 0:

            @pl.when(has_low)
            def _():
                middle[1].start()

        if (base + tiles) * TILE == extent:

            @pl.when(has_high)
            def _():
                middle[0].start()

        for start, rows in jobs2[index]:
            if start < TILE:

                @pl.when(has_low)
                def _():
                    middle[0].wait_recv()

            if start + rows + TILE > extent:

                @pl.when(has_high)
                def _():
                    middle[1].wait_recv()

            after(start, rows)

    @pl.when(has_high)
    def _():
        for upward, _ in edges:
            upward.wait_send()
        middle[0].wait_send()

    @pl.when(has_low)
    def _():
        for _, downward in edges:
            downward.wait_send()
        middle[1].wait_send()

    for copies, _ in plans:
        for copy in copies:
            copy.wait_send()


def on_device(state, forcing, parents, taper_index):
    per_dev, extent, width = state.shape
    patch_dev = extent // PATCH_ROWS
    bands, groups = lax.axis_size("band"), lax.axis_size("pgroup")
    me = lax.axis_index("pgroup")
    lanes = 128

    table = parents.reshape(patch_dev, groups, per_dev)
    within = table - me * per_dev
    mine = (within >= 0) & (within < per_dev)
    least = jnp.min(jnp.where(mine, within, per_dev - 1), axis=2)
    most = jnp.max(jnp.where(mine, within, 0), axis=2)
    chosen = jnp.stack([least, most], axis=2).reshape(-1)
    own = lax.dynamic_index_in_dim(table, me, 1, keepdims=False)
    source = own // per_dev
    other = (source[:, :, None] == source[:, None, :]) & (own[:, None, :] < own[:, :, None])
    rank = jnp.any(other, axis=2).astype(jnp.int32)
    picks = jnp.stack([source, rank], axis=2).reshape(-1)
    taper = jnp.broadcast_to(taper_index.astype(jnp.float32)[:, None], (extent, lanes))

    quarter = extent // TILE // 4
    part = quarter * TILE
    chunks = [(quarter, quarter), (0, quarter), (3 * quarter, quarter), (2 * quarter, quarter)]
    jobs1 = [[(base * TILE, part)] for base, _ in chunks]
    jobs2 = [
        [],
        [],
        [(0, part), (part, part - TILE), (4 * part - TILE, TILE)],
        [(2 * part - TILE, part), (3 * part - TILE, part)],
    ]
    f32 = jnp.float32
    edge = (per_dev, TILE, width)
    buffers = [
        pltpu.VMEM((groups, tiles, CAP, TILE, width), f32) for _, tiles in chunks
    ]
    vmem, smem = pl.BlockSpec(memory_space=pltpu.VMEM), pl.BlockSpec(memory_space=pltpu.SMEM)
    return pl.pallas_call(
        functools.partial(kernel, bands, groups, chunks, jobs1, jobs2),
        out_shape=jax.ShapeDtypeStruct(state.shape, f32),
        in_specs=[vmem, vmem, vmem, smem, smem],
        out_specs=vmem,
        scratch_shapes=[
            pltpu.VMEM(state.shape, f32),
            pltpu.VMEM(state.shape, f32),
            pltpu.VMEM(edge, f32),
            pltpu.VMEM(edge, f32),
            pltpu.VMEM((TILE, width), f32),
            pltpu.VMEM((TILE, width), f32),
            pltpu.VMEM((TILE, lanes), f32),
            pltpu.VMEM((TILE, lanes), f32),
            pltpu.VMEM(edge, f32),
            pltpu.VMEM(edge, f32),
            pltpu.SemaphoreType.DMA((8,)),
            pltpu.SemaphoreType.DMA((8,)),
            pltpu.SemaphoreType.DMA((len(chunks), groups - 1)),
            pltpu.SemaphoreType.DMA((len(chunks), groups - 1)),
            pltpu.SemaphoreType.DMA((len(chunks),)),
            *buffers,
            *buffers,
        ],
        compiler_params=pltpu.CompilerParams(
            collective_id=0, has_side_effects=True, vmem_limit_bytes=56 << 20
        ),
        name="filter_step",
    )(state, forcing, taper, chosen, picks)


def solution(mesh):
    return jax.shard_map(
        on_device,
        mesh=mesh,
        in_specs=(P("pgroup", "band", None), P("band", None), P("band", None), P("band")),
        out_specs=P("pgroup", "band", None),
        check_vma=False,
    )
```

```python
import functools

import jax
import jax.numpy as jnp
from jax import lax
from jax.experimental import pallas as pl
from jax.experimental.pallas import tpu as pltpu
from jax.sharding import PartitionSpec as P

PATCH_ROWS = 4
STEPS = 6
CAP = 2
LANES = 128
TILE = 8
MESH = pl.DeviceIdType.MESH


SCALE = 0.05


def step_rows(c, n, s, drive):
    width = c.shape[-1]
    east = pltpu.roll(c, width - 1, c.ndim - 1)
    west = pltpu.roll(c, 1, c.ndim - 1)
    return (c * (0.4 - (east - west)) + 0.15 * (east + west)) + ((0.05 * n + 0.25 * s) + drive)


def kernel(
    bands, groups, chunks, jobs1, jobs2,
    state, forcing, taper, chosen, picks, out,
    first, resampled, ping, pong, drive, weight,
    s_lo, s_hi, f_lo, f_hi, t_lo, t_hi, r_lo, r_hi,
    halo_send, halo_recv, send_sem, recv_sem, own_sem,
    *buffers,
):
    count = len(chunks)
    sends, recvs = buffers[:count], buffers[count:]
    band = lax.axis_index("band")
    me = lax.axis_index("pgroup")
    per_dev, extent, width = state.shape[0], state.shape[1] * TILE, state.shape[2] * LANES
    has_low, has_high = band > 0, band < bands - 1
    up, down = lax.rem(band + 1, bands), lax.rem(band + bands - 1, bands)

    barrier = pltpu.get_barrier_semaphore()
    for step in range(1, groups):
        pl.semaphore_signal(
            barrier, inc=1, device_id={"pgroup": lax.rem(me + step, groups)}, device_id_type=MESH
        )

    @pl.when(has_low)
    def _():
        pl.semaphore_signal(barrier, inc=1, device_id={"band": down}, device_id_type=MESH)

    @pl.when(has_high)
    def _():
        pl.semaphore_signal(barrier, inc=1, device_id={"band": up}, device_id_type=MESH)

    def halo(index, src, low, high):
        if len(src.shape) == 5:
            last, start = (slice(None), slice(src.shape[1] - 1, None)), (slice(None), slice(0, 1))
        else:
            last, start = (slice(extent - TILE, extent),), (slice(0, TILE),)
        upward = pltpu.make_async_remote_copy(
            src_ref=src.at[last], dst_ref=low,
            send_sem=halo_send.at[2 * index], recv_sem=halo_recv.at[2 * index],
            device_id={"band": up}, device_id_type=MESH,
        )
        downward = pltpu.make_async_remote_copy(
            src_ref=src.at[start], dst_ref=high,
            send_sem=halo_send.at[2 * index + 1], recv_sem=halo_recv.at[2 * index + 1],
            device_id={"band": down}, device_id_type=MESH,
        )
        return upward, downward

    edges = [
        halo(0, state, s_lo, s_hi),
        halo(1, forcing, f_lo, f_hi),
        halo(2, taper, t_lo, t_hi),
    ]
    middle = halo(3, resampled, r_lo, r_hi)

    @pl.when(jnp.logical_not(has_low))
    def _():
        for ref in (s_lo, f_lo, t_lo, r_lo):
            ref[...] = jnp.zeros_like(ref)

    @pl.when(jnp.logical_not(has_high))
    def _():
        for ref in (s_hi, f_hi, t_hi, r_hi):
            ref[...] = jnp.zeros_like(ref)

    packs = per_dev // TILE

    def rows_of(ref, pack, row):
        flat, places, stride = lines(ref, pack, row)
        return jnp.concatenate(
            [flat[pl.ds(place, TILE, stride=stride), :] for place in places], axis=1
        )

    def lines(ref, pack, row):
        blocks = ref.shape[2]
        per = ref.shape[1] * blocks * TILE
        places = [
            pack * (TILE * per) + ((row // TILE) * blocks + b) * TILE + row % TILE
            for b in range(blocks)
        ]
        return ref.reshape(per_dev * per, LANES), places, per

    def piece(low, mid, high, row):
        if row < 0:
            return low, row + TILE
        if row >= extent:
            return high, row - extent
        return mid, row

    def fill(low, high):
        for row in range(low, high):
            ref, at = piece(f_lo, forcing, f_hi, row)
            line = SCALE * ref[pl.ds(at, 1), :]
            drive[row + TILE] = jnp.broadcast_to(line, (TILE, width))
            ref, at = piece(t_lo, taper, t_hi, row)
            kind = jnp.broadcast_to(ref[pl.ds(at, 1), :], (TILE, ref.shape[1])) + 1.0
            near, far = jnp.exp(-0.2 * kind), jnp.exp(-0.8 * kind)
            scale = 1.0 / (1.0 + 2.0 * near + 2.0 * far)
            weight[0, row + TILE] = scale
            weight[1, row + TILE] = near * scale
            weight[2, row + TILE] = far * scale

    def clear(ref, low, high):
        if low < 0:

            @pl.when(jnp.logical_not(has_low))
            def _():
                ref[:, TILE - 1] = jnp.zeros((packs, TILE, width), jnp.float32)

        if high > extent:

            @pl.when(jnp.logical_not(has_high))
            def _():
                ref[:, TILE + extent] = jnp.zeros((packs, TILE, width), jnp.float32)

    def sweep(start, rows, finish):
        source, target = ping, pong
        for step in range(STEPS):
            margin = STEPS - 1 - step
            low, high = start - margin, start + rows + margin
            parts = 2
            size = (high - low) // parts

            def body(i, carry, low=low, size=size, source=source, target=target, last=margin == 0):
                pack, part = i // parts, i % parts
                at = low + TILE + part * size
                u = step_rows(
                    source[pack, pl.ds(at, size)],
                    source[pack, pl.ds(at + 1, size)],
                    source[pack, pl.ds(at - 1, size)],
                    drive[pl.ds(at, size)],
                )
                if last:
                    for r in range(size):
                        finish(pack, at - TILE + r, u[r])
                else:
                    target[pack, pl.ds(at, size)] = u
                return carry

            lax.fori_loop(0, packs * parts, body, 0)
            if margin:
                clear(target, low, high)
            source, target = target, source

    def put(ref, factor):
        def finish(pack, row, value):
            if factor is not None:
                value = value * factor
            flat, places, stride = lines(ref, pack, row)
            for b, place in enumerate(places):
                flat[pl.ds(place, TILE, stride=stride), :] = value[:, b * LANES : (b + 1) * LANES]

        return finish

    def before(start, rows):
        def load(pack, carry):
            for row in range(start - STEPS, start + rows + STEPS):
                ref, at = piece(s_lo, state, s_hi, row)
                ping[pack, row + TILE] = SCALE * rows_of(ref, pack, at)
            return carry

        lax.fori_loop(0, packs, load, 0)
        sweep(start, rows, put(first, None))

    def after(start, rows):
        low, high = start - STEPS, start + rows + STEPS
        repeat = width // taper.shape[1]

        def load(pack, carry):
            near = []
            for row in range(low - 2, high + 2):
                ref, at = piece(r_lo, resampled, r_hi, row)
                near.append(rows_of(ref, pack, at))
            for i, row in enumerate(range(low, high)):
                w0, w1, w2 = (
                    jnp.concatenate([weight[j, row + TILE]] * repeat, axis=1) for j in range(3)
                )
                ping[pack, row + TILE] = (
                    w0 * near[i + 2]
                    + w1 * (near[i + 1] + near[i + 3])
                    + w2 * (near[i] + near[i + 4])
                )
            return carry

        lax.fori_loop(0, packs, load, 0)
        clear(ping, low, high)
        sweep(start, rows, put(out, 1.0 / SCALE))

    shifts = sorted(range(1, groups), key=lambda i: -min(i, groups - i))

    def exchange(index):
        copies = []
        for shift in shifts:
            copies.append(
                pltpu.make_async_remote_copy(
                    src_ref=sends[index].at[lax.rem(me + shift, groups)],
                    dst_ref=recvs[index].at[me],
                    send_sem=send_sem.at[index, shift - 1],
                    recv_sem=recv_sem.at[index, shift - 1],
                    device_id={"pgroup": lax.rem(me + shift, groups)},
                    device_id_type=MESH,
                )
            )
        own = pltpu.make_async_copy(sends[index].at[me], recvs[index].at[me], own_sem.at[index])
        return copies, own

    blocks = width // LANES
    upper = lax.broadcasted_iota(jnp.int32, (blocks, TILE, LANES), 1) < PATCH_ROWS

    def gather(index):
        base, tiles = chunks[index]
        send = sends[index]

        def body(g, carry):
            for j in range(tiles):
                for slot in range(CAP):
                    at = ((2 * (base + j)) * groups + g) * CAP + slot
                    even, odd = chosen[at], chosen[at + groups * CAP]
                    send[g, j, slot] = jnp.where(
                        upper, first[even, base + j], first[odd, base + j]
                    )
            return carry

        lax.fori_loop(0, groups, body, 0)

    def scatter(index):
        base, tiles = chunks[index]
        recv = recvs[index]

        def body(k, carry):
            for j in range(tiles):
                at = ((2 * (base + j)) * per_dev + k) * 2
                even = recv[picks[at], j, picks[at + 1]]
                odd = recv[picks[at + 2 * per_dev], j, picks[at + 2 * per_dev + 1]]
                resampled[k, base + j] = jnp.where(upper, even, odd)
            return carry

        lax.fori_loop(0, per_dev, body, 0)

    fill(0, extent)
    plans = [exchange(index) for index in range(count)]
    for index in range(count):
        for start, rows in jobs1[index]:
            before(start, rows)
        gather(index)
        if index == 0:
            pl.semaphore_wait(
                barrier, groups - 1 + has_low.astype(jnp.int32) + has_high.astype(jnp.int32)
            )

            @pl.when(has_high)
            def _():
                for upward, _ in edges:
                    upward.start()

            @pl.when(has_low)
            def _():
                for _, downward in edges:
                    downward.start()

        copies, own = plans[index]
        for copy in copies:
            copy.start()
        own.start()
        if index == 0:

            @pl.when(has_low)
            def _():
                for upward, _ in edges:
                    upward.wait_recv()

            @pl.when(has_high)
            def _():
                for _, downward in edges:
                    downward.wait_recv()

            fill(-TILE, 0)
            fill(extent, extent + TILE)

    for index in range(count):
        copies, own = plans[index]
        for copy in copies:
            copy.wait_recv()
        own.wait()
        scatter(index)
        base, tiles = chunks[index]
        if base == 0:

            @pl.when(has_low)
            def _():
                middle[1].start()

        if (base + tiles) * TILE == extent:

            @pl.when(has_high)
            def _():
                middle[0].start()

        for start, rows in jobs2[index]:
            if start < TILE:

                @pl.when(has_low)
                def _():
                    middle[0].wait_recv()

            if start + rows + TILE > extent:

                @pl.when(has_high)
                def _():
                    middle[1].wait_recv()

            after(start, rows)

    @pl.when(has_high)
    def _():
        for upward, _ in edges:
            upward.wait_send()
        middle[0].wait_send()

    @pl.when(has_low)
    def _():
        for _, downward in edges:
            downward.wait_send()
        middle[1].wait_send()

    for copies, _ in plans:
        for copy in copies:
            copy.wait_send()


def on_device(state, forcing, parents, taper_index):
    per_dev, extent, width = state.shape
    patch_dev = extent // PATCH_ROWS
    bands, groups = lax.axis_size("band"), lax.axis_size("pgroup")
    me = lax.axis_index("pgroup")
    lanes = LANES
    blocks, row_tiles = width // lanes, extent // TILE
    state = state.reshape(per_dev, row_tiles, TILE, blocks, lanes).transpose(0, 1, 3, 2, 4)

    table = parents.reshape(patch_dev, groups, per_dev)
    within = table - me * per_dev
    mine = (within >= 0) & (within < per_dev)
    least = jnp.min(jnp.where(mine, within, per_dev - 1), axis=2)
    most = jnp.max(jnp.where(mine, within, 0), axis=2)
    chosen = jnp.stack([least, most], axis=2).reshape(-1)
    own = lax.dynamic_index_in_dim(table, me, 1, keepdims=False)
    source = own // per_dev
    other = (source[:, :, None] == source[:, None, :]) & (own[:, None, :] < own[:, :, None])
    rank = jnp.any(other, axis=2).astype(jnp.int32)
    picks = jnp.stack([source, rank], axis=2).reshape(-1)
    taper = jnp.broadcast_to(taper_index.astype(jnp.float32)[:, None], (extent, lanes))

    quarter = extent // TILE // 4
    part = quarter * TILE
    chunks = [(quarter, quarter), (0, quarter), (3 * quarter, quarter), (2 * quarter, quarter)]
    jobs1 = [[(base * TILE, part)] for base, _ in chunks]
    jobs2 = [
        [],
        [],
        [(0, 2 * part - TILE), (4 * part - TILE, TILE)],
        [(2 * part - TILE, part), (3 * part - TILE, part)],
    ]
    f32 = jnp.float32
    edge = (per_dev, 1, blocks, TILE, lanes)
    buffers = [
        pltpu.VMEM((groups, tiles, CAP, blocks, TILE, lanes), f32) for _, tiles in chunks
    ]
    vmem, smem = pl.BlockSpec(memory_space=pltpu.VMEM), pl.BlockSpec(memory_space=pltpu.SMEM)
    out = pl.pallas_call(
        functools.partial(kernel, bands, groups, chunks, jobs1, jobs2),
        out_shape=jax.ShapeDtypeStruct(state.shape, f32),
        in_specs=[vmem, vmem, vmem, smem, smem],
        out_specs=vmem,
        scratch_shapes=[
            pltpu.VMEM(state.shape, f32),
            pltpu.VMEM(state.shape, f32),
            pltpu.VMEM((per_dev // TILE, extent + 2 * TILE, TILE, width), f32),
            pltpu.VMEM((per_dev // TILE, extent + 2 * TILE, TILE, width), f32),
            pltpu.VMEM((extent + 2 * TILE, TILE, width), f32),
            pltpu.VMEM((3, extent + 2 * TILE, TILE, lanes), f32),
            pltpu.VMEM(edge, f32),
            pltpu.VMEM(edge, f32),
            pltpu.VMEM((TILE, width), f32),
            pltpu.VMEM((TILE, width), f32),
            pltpu.VMEM((TILE, lanes), f32),
            pltpu.VMEM((TILE, lanes), f32),
            pltpu.VMEM(edge, f32),
            pltpu.VMEM(edge, f32),
            pltpu.SemaphoreType.DMA((8,)),
            pltpu.SemaphoreType.DMA((8,)),
            pltpu.SemaphoreType.DMA((len(chunks), groups - 1)),
            pltpu.SemaphoreType.DMA((len(chunks), groups - 1)),
            pltpu.SemaphoreType.DMA((len(chunks),)),
            *buffers,
            *buffers,
        ],
        compiler_params=pltpu.CompilerParams(
            collective_id=0, has_side_effects=True, vmem_limit_bytes=56 << 20
        ),
        name="filter_step",
    )(state, forcing, taper, chosen, picks)
    return out.transpose(0, 1, 3, 2, 4).reshape(per_dev, extent, width)


def solution(mesh):
    return jax.shard_map(
        on_device,
        mesh=mesh,
        in_specs=(P("pgroup", "band", None), P("band", None), P("band", None), P("band")),
        out_specs=P("pgroup", "band", None),
        check_vma=False,
    )
```

```python
import functools

import jax
import jax.numpy as jnp
from jax import lax
from jax.experimental import pallas as pl
from jax.experimental.pallas import tpu as pltpu
from jax.sharding import PartitionSpec as P

PATCH_ROWS = 4
STEPS = 6
CAP = 2
LANES = 128
TILE = 8
MESH = pl.DeviceIdType.MESH


SCALE = 0.05


def step_rows(c, n, s, drive):
    width = c.shape[-1]
    east = pltpu.roll(c, width - 1, c.ndim - 1)
    west = pltpu.roll(c, 1, c.ndim - 1)
    return (c * (0.4 - (east - west)) + 0.15 * (east + west)) + ((0.05 * n + 0.25 * s) + drive)


def kernel(
    bands, groups, chunks, jobs1, jobs2,
    state, forcing, taper, least, most, source, rank, out,
    first, resampled, ping, pong, drive, weight,
    s_lo, s_hi, f_lo, f_hi, t_lo, t_hi, r_lo, r_hi,
    halo_send, halo_recv, send_sem, recv_sem, own_sem,
    *buffers,
):
    count = len(chunks)
    sends, recvs = buffers[:count], buffers[count:]
    band = lax.axis_index("band")
    me = lax.axis_index("pgroup")
    per_dev, extent, width = state.shape[0], state.shape[1] * TILE, state.shape[2] * LANES
    has_low, has_high = band > 0, band < bands - 1
    up, down = lax.rem(band + 1, bands), lax.rem(band + bands - 1, bands)

    barrier = pltpu.get_barrier_semaphore()
    for step in range(1, groups):
        pl.semaphore_signal(
            barrier, inc=1, device_id={"pgroup": lax.rem(me + step, groups)}, device_id_type=MESH
        )

    @pl.when(has_low)
    def _():
        pl.semaphore_signal(barrier, inc=1, device_id={"band": down}, device_id_type=MESH)

    @pl.when(has_high)
    def _():
        pl.semaphore_signal(barrier, inc=1, device_id={"band": up}, device_id_type=MESH)

    def halo(index, src, low, high):
        if len(src.shape) == 5:
            last, start = (slice(None), slice(src.shape[1] - 1, None)), (slice(None), slice(0, 1))
        else:
            last, start = (slice(extent - TILE, extent),), (slice(0, TILE),)
        upward = pltpu.make_async_remote_copy(
            src_ref=src.at[last], dst_ref=low,
            send_sem=halo_send.at[2 * index], recv_sem=halo_recv.at[2 * index],
            device_id={"band": up}, device_id_type=MESH,
        )
        downward = pltpu.make_async_remote_copy(
            src_ref=src.at[start], dst_ref=high,
            send_sem=halo_send.at[2 * index + 1], recv_sem=halo_recv.at[2 * index + 1],
            device_id={"band": down}, device_id_type=MESH,
        )
        return upward, downward

    edges = [
        halo(0, state, s_lo, s_hi),
        halo(1, forcing, f_lo, f_hi),
        halo(2, taper, t_lo, t_hi),
    ]
    middle = halo(3, resampled, r_lo, r_hi)

    @pl.when(jnp.logical_not(has_low))
    def _():
        for ref in (s_lo, f_lo, t_lo, r_lo):
            ref[...] = jnp.zeros_like(ref)

    @pl.when(jnp.logical_not(has_high))
    def _():
        for ref in (s_hi, f_hi, t_hi, r_hi):
            ref[...] = jnp.zeros_like(ref)

    packs = per_dev // TILE

    def rows_of(ref, pack, row):
        flat, places, stride = lines(ref, pack, row)
        return jnp.concatenate(
            [flat[pl.ds(place, TILE, stride=stride), :] for place in places], axis=1
        )

    def lines(ref, pack, row):
        blocks = ref.shape[2]
        per = ref.shape[1] * blocks * TILE
        places = [
            pack * (TILE * per) + ((row // TILE) * blocks + b) * TILE + row % TILE
            for b in range(blocks)
        ]
        return ref.reshape(per_dev * per, LANES), places, per

    def piece(low, mid, high, row):
        if row < 0:
            return low, row + TILE
        if row >= extent:
            return high, row - extent
        return mid, row

    def fill_drive(low, high):
        for row in range(low, high):
            ref, at = piece(f_lo, forcing, f_hi, row)
            line = SCALE * ref[pl.ds(at, 1), :]
            drive[row + TILE] = jnp.broadcast_to(line, (TILE, width))

    def fill_weight(low, high):
        for row in range(low, high):
            ref, at = piece(t_lo, taper, t_hi, row)
            kind = jnp.broadcast_to(ref[pl.ds(at, 1), :], (TILE, ref.shape[1])) + 1.0
            near, far = jnp.exp(-0.2 * kind), jnp.exp(-0.8 * kind)
            scale = 1.0 / (1.0 + 2.0 * near + 2.0 * far)
            weight[0, row + TILE] = scale
            weight[1, row + TILE] = near * scale
            weight[2, row + TILE] = far * scale

    def clear(ref, low, high):
        if low < 0:

            @pl.when(jnp.logical_not(has_low))
            def _():
                ref[:, TILE - 1] = jnp.zeros((packs, TILE, width), jnp.float32)

        if high > extent:

            @pl.when(jnp.logical_not(has_high))
            def _():
                ref[:, TILE + extent] = jnp.zeros((packs, TILE, width), jnp.float32)

    def sweep(start, rows, finish):
        source, target = ping, pong
        for step in range(STEPS):
            margin = STEPS - 1 - step
            low, high = start - margin, start + rows + margin
            parts = 1
            size = (high - low) // parts

            def body(i, carry, low=low, size=size, source=source, target=target, last=margin == 0):
                pack, part = i // parts, i % parts
                at = low + TILE + part * size
                u = step_rows(
                    source[pack, pl.ds(at, size)],
                    source[pack, pl.ds(at + 1, size)],
                    source[pack, pl.ds(at - 1, size)],
                    drive[pl.ds(at, size)],
                )
                if last:
                    for r in range(size):
                        finish(pack, at - TILE + r, u[r])
                else:
                    target[pack, pl.ds(at, size)] = u
                return carry

            lax.fori_loop(0, packs * parts, body, 0)
            if margin:
                clear(target, low, high)
            source, target = target, source

    def put(ref, factor):
        def finish(pack, row, value):
            if factor is not None:
                value = value * factor
            flat, places, stride = lines(ref, pack, row)
            for b, place in enumerate(places):
                flat[pl.ds(place, TILE, stride=stride), :] = value[:, b * LANES : (b + 1) * LANES]

        return finish

    def before(start, rows):
        def load(pack, carry):
            for row in range(start - STEPS, start + rows + STEPS):
                ref, at = piece(s_lo, state, s_hi, row)
                ping[pack, row + TILE] = SCALE * rows_of(ref, pack, at)
            return carry

        lax.fori_loop(0, packs, load, 0)
        sweep(start, rows, put(first, None))

    def after(start, rows):
        low, high = start - STEPS, start + rows + STEPS
        repeat = width // taper.shape[1]

        def load(pack, carry):
            near = []
            for row in range(low - 2, high + 2):
                ref, at = piece(r_lo, resampled, r_hi, row)
                near.append(rows_of(ref, pack, at))
            for i, row in enumerate(range(low, high)):
                w0, w1, w2 = (
                    jnp.concatenate([weight[j, row + TILE]] * repeat, axis=1) for j in range(3)
                )
                ping[pack, row + TILE] = (
                    w0 * near[i + 2]
                    + w1 * (near[i + 1] + near[i + 3])
                    + w2 * (near[i] + near[i + 4])
                )
            return carry

        lax.fori_loop(0, packs, load, 0)
        clear(ping, low, high)
        sweep(start, rows, put(out, None))

    shifts = sorted(range(1, groups), key=lambda i: -min(i, groups - i))

    def exchange(index):
        copies = []
        for shift in shifts:
            copies.append(
                pltpu.make_async_remote_copy(
                    src_ref=sends[index].at[lax.rem(me + shift, groups)],
                    dst_ref=recvs[index].at[me],
                    send_sem=send_sem.at[index, shift - 1],
                    recv_sem=recv_sem.at[index, shift - 1],
                    device_id={"pgroup": lax.rem(me + shift, groups)},
                    device_id_type=MESH,
                )
            )
        own = pltpu.make_async_copy(sends[index].at[me], recvs[index].at[me], own_sem.at[index])
        return copies, own

    blocks = width // LANES
    upper = lax.broadcasted_iota(jnp.int32, (blocks, TILE, LANES), 1) < PATCH_ROWS

    def gather(index):
        base, tiles = chunks[index]
        send = sends[index]

        def body(g, carry):
            for j in range(tiles):
                for slot, table in enumerate((least, most)):
                    even, odd = table[2 * (base + j), g], table[2 * (base + j) + 1, g]
                    send[g, j, slot] = jnp.where(
                        upper, first[even, base + j], first[odd, base + j]
                    )
            return carry

        lax.fori_loop(0, groups, body, 0)

    def scatter(index):
        base, tiles = chunks[index]
        recv = recvs[index]

        def body(k, carry):
            for j in range(tiles):
                at = 2 * (base + j)
                even = recv[source[at, k], j, rank[at, k]]
                odd = recv[source[at + 1, k], j, rank[at + 1, k]]
                resampled[k, base + j] = jnp.where(upper, even, odd)
            return carry

        lax.fori_loop(0, per_dev, body, 0)

    fill_drive(0, extent)
    plans = [exchange(index) for index in range(count)]
    for index in range(count):
        for start, rows in jobs1[index]:
            before(start, rows)
        gather(index)
        if index == 0:
            pl.semaphore_wait(
                barrier, groups - 1 + has_low.astype(jnp.int32) + has_high.astype(jnp.int32)
            )

            @pl.when(has_high)
            def _():
                for upward, _ in edges:
                    upward.start()

            @pl.when(has_low)
            def _():
                for _, downward in edges:
                    downward.start()

        copies, own = plans[index]
        for copy in copies:
            copy.start()
        own.start()
        if index == 1:

            @pl.when(has_low)
            def _():
                for upward, _ in edges:
                    upward.wait_recv()

            @pl.when(has_high)
            def _():
                for _, downward in edges:
                    downward.wait_recv()

            fill_drive(-TILE, 0)
            fill_drive(extent, extent + TILE)
            fill_weight(-TILE, extent + TILE)

    for index in range(count):
        copies, own = plans[index]
        for copy in copies:
            copy.wait_recv()
        own.wait()
        scatter(index)
        base, tiles = chunks[index]
        if base == 0:

            @pl.when(has_low)
            def _():
                middle[1].start()

        if (base + tiles) * TILE == extent:

            @pl.when(has_high)
            def _():
                middle[0].start()

        for start, rows in jobs2[index]:
            if start < TILE:

                @pl.when(has_low)
                def _():
                    middle[0].wait_recv()

            if start + rows + TILE > extent:

                @pl.when(has_high)
                def _():
                    middle[1].wait_recv()

            after(start, rows)

    @pl.when(has_high)
    def _():
        for upward, _ in edges:
            upward.wait_send()
        middle[0].wait_send()

    @pl.when(has_low)
    def _():
        for _, downward in edges:
            downward.wait_send()
        middle[1].wait_send()

    for copies, _ in plans:
        for copy in copies:
            copy.wait_send()


def on_device(state, forcing, parents, taper_index):
    per_dev, extent, width = state.shape
    patch_dev = extent // PATCH_ROWS
    bands, groups = lax.axis_size("band"), lax.axis_size("pgroup")
    me = lax.axis_index("pgroup")
    lanes = LANES
    blocks, row_tiles = width // lanes, extent // TILE
    state = state.reshape(per_dev, row_tiles, TILE, blocks, lanes).transpose(0, 1, 3, 2, 4)

    table = parents.reshape(patch_dev, groups, per_dev)
    within = table - me * per_dev
    mine = (within >= 0) & (within < per_dev)
    least = jnp.min(jnp.where(mine, within, per_dev - 1), axis=2)
    most = jnp.max(jnp.where(mine, within, 0), axis=2)
    own = lax.dynamic_index_in_dim(table, me, 1, keepdims=False)
    source = own // per_dev
    other = (source[:, :, None] == source[:, None, :]) & (own[:, None, :] < own[:, :, None])
    rank = jnp.any(other, axis=2).astype(jnp.int32)
    taper = jnp.broadcast_to(taper_index.astype(jnp.float32)[:, None], (extent, lanes))

    quarter = extent // TILE // 4
    part = quarter * TILE
    chunks = [
        (2 * quarter - 1, 1),
        (quarter, quarter - 1),
        (0, quarter),
        (3 * quarter, quarter),
        (2 * quarter, quarter - 1),
        (3 * quarter - 1, 1),
    ]
    jobs1 = [[(base * TILE, tiles * TILE)] for base, tiles in chunks]
    jobs2 = [
        [],
        [],
        [(TILE, 2 * part - 2 * TILE)],
        [],
        [(2 * part - TILE, part - TILE), (0, TILE), (4 * part - TILE, TILE)],
        [(3 * part - 2 * TILE, 3 * TILE)],
    ]
    f32 = jnp.float32
    edge = (per_dev, 1, blocks, TILE, lanes)
    buffers = [
        pltpu.VMEM((groups, tiles, CAP, blocks, TILE, lanes), f32) for _, tiles in chunks
    ]
    vmem, smem = pl.BlockSpec(memory_space=pltpu.VMEM), pl.BlockSpec(memory_space=pltpu.SMEM)
    out = pl.pallas_call(
        functools.partial(kernel, bands, groups, chunks, jobs1, jobs2),
        out_shape=jax.ShapeDtypeStruct(state.shape, f32),
        in_specs=[vmem, vmem, vmem, smem, smem, smem, smem],
        out_specs=vmem,
        scratch_shapes=[
            pltpu.VMEM(state.shape, f32),
            pltpu.VMEM(state.shape, f32),
            pltpu.VMEM((per_dev // TILE, extent + 2 * TILE, TILE, width), f32),
            pltpu.VMEM((per_dev // TILE, extent + 2 * TILE, TILE, width), f32),
            pltpu.VMEM((extent + 2 * TILE, TILE, width), f32),
            pltpu.VMEM((3, extent + 2 * TILE, TILE, lanes), f32),
            pltpu.VMEM(edge, f32),
            pltpu.VMEM(edge, f32),
            pltpu.VMEM((TILE, width), f32),
            pltpu.VMEM((TILE, width), f32),
            pltpu.VMEM((TILE, lanes), f32),
            pltpu.VMEM((TILE, lanes), f32),
            pltpu.VMEM(edge, f32),
            pltpu.VMEM(edge, f32),
            pltpu.SemaphoreType.DMA((8,)),
            pltpu.SemaphoreType.DMA((8,)),
            pltpu.SemaphoreType.DMA((len(chunks), groups - 1)),
            pltpu.SemaphoreType.DMA((len(chunks), groups - 1)),
            pltpu.SemaphoreType.DMA((len(chunks),)),
            *buffers,
            *buffers,
        ],
        compiler_params=pltpu.CompilerParams(
            collective_id=0, has_side_effects=True, vmem_limit_bytes=56 << 20
        ),
        name="filter_step",
    )(state, forcing, taper, least, most, source, rank)
    out = out * (1.0 / SCALE)
    return out.transpose(0, 1, 3, 2, 4).reshape(per_dev, extent, width)


def solution(mesh):
    return jax.shard_map(
        on_device,
        mesh=mesh,
        in_specs=(P("pgroup", "band", None), P("band", None), P("band", None), P("band")),
        out_specs=P("pgroup", "band", None),
        check_vma=False,
    )
```
